256 devices in a mesh: freq: 4 (over y_hi, core), sub: 64 (over x, z, y_lo).
Axes of the slice: x: 4, y: 4 (y_hi: 2, y_lo: 2; y = y_hi * 2 + y_lo), z: 8, core: 2. Of those that a mesh axis runs over, the one named last changes fastest.
Arguments:
- impedance: float32 [4, 64, 1280, 1280], P('freq', 'sub'), may hold values from -0.125 to 0.125
- interior_map: bfloat16 [4, 64, 2048, 1280], P('freq', 'sub'), may hold values from -6 to 6
- source_cells: int32 [128], replicated, may hold values from 0 to 65535
- receiver_cells: int32 [128], replicated, may hold values from 0 to 65535
Outputs:
- hessian: float32 [64, 1024, 1024], P('sub', 'freq')
The draws below stay inside these ranges and needn't reach their ends.
All inputs are finite; a program needn't handle non-finite values.
Results may differ from the reference program's by a relative error of at most 0.0059.
Values may be sent and summed in bfloat16 or wider, within the bound.
A program may use at most 64 MiB of HBM per device.

```python
import jax
import jax.numpy as jnp
from jax import lax

CX = 8
CY = 8
CZ = 16
NSRC = 128
NRCV = 128
SWEEPS = 3
CELLS = 1024
FACES = 640
TRACE = 1280
RHS = 256
SGX = 4
SGY = 4
SGZ = 4
SUBS = 64
FREQS = 4


def set_ends(drawn, own_key, least, largest):
    dims = drawn.shape
    place = [jax.random.randint(jax.random.fold_in(own_key, axis), (), 0, dims[axis]) for axis in range(len(dims))]
    drawn = drawn.at[tuple(place)].set(least)
    longest = dims.index(max(dims))
    place[longest] = (place[longest] + 1) % dims[longest]
    return drawn.at[tuple(place)].set(largest)


def block_scale(key, extent, shards, smallest, top_value):
    def one(position, shards_of):
        heights = jax.random.uniform(jax.random.fold_in(jax.random.fold_in(key, 6), position), (shards_of,), jnp.float32, smallest / len(shards), top_value / len(shards))
        return jnp.repeat(jnp.exp(heights), extent[position] // shards_of).reshape((-1,) + (1,) * (len(extent) - position - 1))

    factor_of = one(*shards[0])
    for cut in shards[1:]:
        factor_of = factor_of * one(*cut)
    return factor_of


def noise(own_key, extent, scale, limit, cuts=(), held_as=jnp.bfloat16):
    entries = scale * jax.random.normal(own_key, extent, jnp.float32)
    if cuts:
        entries = entries * block_scale(own_key, extent, cuts, -0.22, 0.18)
    return jnp.clip(entries, -limit, limit).astype(held_as)


def setup_inputs(seed: int = 0) -> dict:
    splits = jax.random.split(jax.random.key(seed), 5)
    impedance = noise(splits[0], (FREQS, SUBS, TRACE, TRACE), (0.7 * TRACE ** -0.5), 0.125, ((0, 4), (1, 64)), jnp.float32)
    interior_map = noise(splits[1], (FREQS, SUBS, 2 * CELLS, TRACE), 1.0, 6.0, ((0, 4), (1, 64)))
    source_cells = set_ends(jax.random.randint(splits[2], (NSRC,), 0, SUBS * CELLS), jax.random.fold_in(splits[2], 1), 0, (SUBS * CELLS) - 1).astype(jnp.int32)
    receiver_cells = set_ends(jax.random.randint(splits[3], (NRCV,), 0, SUBS * CELLS), jax.random.fold_in(splits[3], 1), 0, (SUBS * CELLS) - 1).astype(jnp.int32)
    return dict(impedance=impedance, interior_map=interior_map, source_cells=source_cells, receiver_cells=receiver_cells)


def face_spans():
    counts = [CY * CZ, CY * CZ, CX * CZ, CX * CZ, CX * CY, CX * CY]
    spans = []
    begin = 0
    for count in counts:
        spans.append((begin, count))
        begin = begin + count
    return spans


def move_along(block, axis_number, forward):
    length = block.shape[axis_number]
    widths = [(0, 0)] * block.ndim
    if forward:
        widths[axis_number] = (1, 0)
        padded = jnp.pad(block, widths)
        return lax.slice_in_dim(padded, 0, length, axis=axis_number)
    widths[axis_number] = (0, 1)
    padded = jnp.pad(block, widths)
    return lax.slice_in_dim(padded, 1, length + 1, axis=axis_number)


def swap_faces(outgoing_trace_values):
    grid = outgoing_trace_values.reshape(SGZ, SGY, SGX, 2, FACES, RHS)
    spans = face_spans()
    axis_of = [2, 2, 1, 1, 0, 0]
    pieces = []
    for face_index in range(6):
        partner = face_index + 1 if face_index % 2 == 0 else face_index - 1
        begin, count = spans[partner]
        piece = grid[:, :, :, :, begin:begin + count, :]
        pieces.append(move_along(piece, axis_of[face_index], face_index % 2 == 0))
    return jnp.concatenate(pieces, axis=4).reshape(SUBS, TRACE, RHS)


def gram_parts(fields, first, count):
    real_part = fields[:CELLS, first:first + count]
    imag_part = fields[CELLS:, first:first + count]
    left = jnp.concatenate([real_part, imag_part], axis=1)
    rotated_block = jnp.concatenate([imag_part, -real_part], axis=1)
    real_gram = jnp.dot(left, left.T, preferred_element_type=jnp.float32)
    imaginary_gram_matrix = jnp.dot(rotated_block, left.T, preferred_element_type=jnp.float32)
    return real_gram, imaginary_gram_matrix


def frequency_core(boundary_impedance_values, interiors, source_global, receiver_global):
    all_cells = jnp.concatenate([source_global, receiver_global]).astype(jnp.int32)
    owner = all_cells // CELLS
    local_cell = (all_cells % CELLS).astype(jnp.int32)
    inside = owner[None, :] == jnp.arange(SUBS, dtype=jnp.int32)[:, None]
    picked = interiors[:, local_cell, :].astype(jnp.float32)
    source_loading = jnp.where(inside[:, :, None], picked, jnp.float32(0.0)).transpose(0, 2, 1)
    incoming_trace_values = jnp.zeros((SUBS, TRACE, RHS), jnp.float32)
    for sweep_index in range(SWEEPS):
        outgoing_trace_values = jnp.einsum("lnu,luk->lnk", boundary_impedance_values, incoming_trace_values, precision=lax.Precision.HIGHEST) + source_loading
        incoming_trace_values = swap_faces(outgoing_trace_values)
    row_ids = jnp.arange(2 * CELLS, dtype=jnp.int32)
    field_scale = jnp.float32(TRACE ** -0.5)

    def rebuild(items):
        interior, trace_in, inside_here = items
        product = jnp.dot(interior, trace_in.astype(jnp.bfloat16), preferred_element_type=jnp.float32)
        point = (row_ids[:, None] == local_cell[None, :]) & inside_here[None, :]
        return (product * field_scale + point.astype(jnp.float32)).astype(jnp.bfloat16)

    return lax.map(rebuild, (interiors, incoming_trace_values, inside))


def reference(impedance, interior_map, source_cells, receiver_cells):
    def per_frequency(operands):
        boundary_impedance_values, interiors = operands
        return frequency_core(boundary_impedance_values, interiors, source_cells, receiver_cells)

    fields = lax.map(per_frequency, (impedance, interior_map))

    def per_subdomain(sub_fields):
        total = jnp.zeros((CELLS, CELLS), jnp.float32)
        for freq_index in range(FREQS):
            real_u, imag_u = gram_parts(sub_fields[freq_index], 0, NSRC)
            real_v, imag_v = gram_parts(sub_fields[freq_index], NSRC, NRCV)
            total = total + (real_u * real_v - imag_u * imag_v) / (NSRC * NRCV)
        return total

    return lax.map(per_subdomain, fields.transpose(1, 0, 2, 3))
```

```python
import jax
import jax.numpy as jnp
from jax import lax
from jax.experimental import pallas as pl
from jax.experimental.pallas import tpu as pltpu
from jax.sharding import PartitionSpec as P

CX = 8
CY = 8
CZ = 16
NSRC = 128
NRCV = 128
SWEEPS = 3
CELLS = 1024
FACES = 640
TRACE = 1280
RHS = 256
ROWS = 256
BLOCKS = CELLS // ROWS
MESH = pl.DeviceIdType.MESH
COUNTS = (CY * CZ, CY * CZ, CX * CZ, CX * CZ, CX * CY, CX * CY)
BEGINS = tuple(sum(COUNTS[:i]) for i in range(6))
PARTNER = (1, 0, 3, 2, 5, 4)
ORDER = (2, 3, 0, 1, 4, 5)
NT = (((1,), (1,)), ((), ()))


def kernel(
    nsub,
    cells_row,
    cells_col,
    z_hbm,
    interior_hbm,
    out_ref,
    zf,
    zb,
    interior,
    inc,
    outb,
    lu,
    ru,
    lv,
    rv,
    send_a,
    recv_a,
    send_y,
    recv_y,
    load_sem,
    face_send,
    face_recv,
    a_send,
    a_recv,
    y_send,
    y_recv,
):
    sub = lax.axis_index("sub")
    freq = lax.axis_index("freq")
    grid_x = min(4, nsub)
    grid_y = min(4, nsub // grid_x)
    grid_z = nsub // (grid_x * grid_y)
    sizes = (grid_x, grid_y, grid_z)
    strides = (1, grid_x, grid_x * grid_y)
    coords = (sub % grid_x, sub // grid_x % grid_y, sub // (grid_x * grid_y))
    valid = []
    beside = []
    for face in range(6):
        axis = face // 2
        if face % 2 == 0:
            valid.append(coords[axis] > 0)
            beside.append(sub - strides[axis])
        else:
            valid.append(coords[axis] < sizes[axis] - 1)
            beside.append(sub + strides[axis])
    chip = freq // 2
    core = freq % 2
    sibling = {"freq": chip * 2 + 1 - core}
    across = {"freq": (1 - chip) * 2 + core}

    def fetch(part):
        rows = pl.ds(part * CELLS, CELLS)
        return pltpu.make_async_copy(interior_hbm.at[rows], interior.at[rows], load_sem.at[part])

    fetch_z = pltpu.make_async_copy(z_hbm, zf, load_sem.at[2])
    fetch(0).start()
    fetch_z.start()
    fetch(1).start()

    barrier = pltpu.get_barrier_semaphore()
    greeted = jnp.int32(2)
    for face in range(6):
        greeted = greeted + valid[face].astype(jnp.int32)

        @pl.when(valid[face])
        def _():
            pl.semaphore_signal(barrier, inc=1, device_id={"sub": beside[face]}, device_id_type=MESH)

    pl.semaphore_signal(barrier, inc=1, device_id=sibling, device_id_type=MESH)
    pl.semaphore_signal(barrier, inc=1, device_id=across, device_id_type=MESH)

    def span(face):
        return pl.ds(BEGINS[face], COUNTS[face])

    for face in range(6):

        @pl.when(jnp.logical_not(valid[face]))
        def _():
            for k in range(SWEEPS):
                inc[k, :, span(face), :] = jnp.zeros((2, COUNTS[face], RHS), jnp.bfloat16)

    def outward(k, face):
        other = PARTNER[face]
        return pltpu.make_async_remote_copy(
            src_ref=outb.at[k, :, span(face), :],
            dst_ref=inc.at[k, :, span(other), :],
            send_sem=face_send.at[k, face],
            recv_sem=face_recv.at[k, other],
            device_id={"sub": beside[face]},
            device_id_type=MESH,
        )

    def inward(k, face):
        return pltpu.make_async_remote_copy(
            src_ref=outb.at[k, :, span(face), :],
            dst_ref=inc.at[k, :, span(face), :],
            send_sem=face_send.at[k, face],
            recv_sem=face_recv.at[k, face],
            device_id={"sub": beside[face]},
            device_id_type=MESH,
        )

    def send(k, face):
        @pl.when(valid[face])
        def _():
            outward(k, face).start()

    def receive(k):
        for face in ORDER:

            @pl.when(valid[face])
            def _():
                inward(k, face).wait_recv()

    first = sub * CELLS
    hot = cells_col[...] == first + lax.broadcasted_iota(jnp.int32, (RHS, CELLS), 1)
    hot = hot.astype(jnp.float32).astype(jnp.bfloat16)
    fetch(0).wait()
    picked = jnp.dot(hot, interior[:CELLS, :], preferred_element_type=jnp.float32)
    load = picked.T.astype(jnp.bfloat16)
    outb[0, 0] = load[:FACES]
    outb[0, 1] = load[FACES:]
    pl.semaphore_wait(barrier, greeted)
    for face in ORDER:
        send(0, face)

    fetch_z.wait()

    @pl.loop(0, TRACE // 128)
    def _(i):
        rows = pl.ds(pl.multiple_of(i * 128, 128), 128)
        zb[rows, :] = zf[rows, :].astype(jnp.bfloat16)

    for k in range(1, SWEEPS):
        receive(k - 1)
        arrived = inc[k - 1].reshape(TRACE, RHS)
        for face in ORDER[::2]:
            begin = BEGINS[face]
            count = COUNTS[face] * 2
            z_rows = jnp.concatenate([zb[begin : begin + count, :], zb[FACES + begin : FACES + begin + count, :]], axis=0)
            product = jnp.dot(z_rows, arrived, preferred_element_type=jnp.float32)
            for part in range(2):
                added = outb[0, part, begin : begin + count, :].astype(jnp.float32)
                total = product[part * count : (part + 1) * count] + added
                outb[k, part, begin : begin + count, :] = total.astype(jnp.bfloat16)
            send(k, face)
            send(k, face + 1)
    fetch(1).wait()
    receive(SWEEPS - 1)

    field_scale = jnp.float32(TRACE ** (-0.5))

    @pl.loop(0, BLOCKS)
    def _(i):
        begin = pl.multiple_of(i * ROWS, ROWS)
        trace = inc[SWEEPS - 1].reshape(TRACE, RHS)
        rows = pl.ds(begin, ROWS)
        real = jnp.dot(interior[rows, :], trace, preferred_element_type=jnp.float32)
        low = pl.ds(pl.multiple_of(CELLS + i * ROWS, ROWS), ROWS)
        imag = jnp.dot(interior[low, :], trace, preferred_element_type=jnp.float32)
        point = cells_row[...] == first + begin + lax.broadcasted_iota(jnp.int32, (ROWS, RHS), 0)
        real = real * field_scale + point.astype(jnp.float32)
        imag = imag * field_scale
        real_b = real.astype(jnp.bfloat16)
        imag_b = imag.astype(jnp.bfloat16)
        minus_b = (-real).astype(jnp.bfloat16)
        lu[rows, :NSRC] = real_b[:, :NSRC]
        lu[rows, NSRC:] = imag_b[:, :NSRC]
        ru[rows, :NSRC] = imag_b[:, :NSRC]
        ru[rows, NSRC:] = minus_b[:, :NSRC]
        lv[rows, :NRCV] = real_b[:, NSRC:]
        lv[rows, NRCV:] = imag_b[:, NSRC:]
        rv[rows, :NRCV] = imag_b[:, NSRC:]
        rv[rows, NRCV:] = minus_b[:, NSRC:]

    def term(owner, j):
        rows = pl.ds(pl.multiple_of(owner * ROWS, ROWS), ROWS)
        cols = pl.ds(pl.multiple_of(j * ROWS, ROWS), ROWS)
        left_u = jnp.concatenate([lu[rows, :], ru[rows, :]], axis=0)
        gram_u = lax.dot_general(left_u, lu[cols, :], NT, preferred_element_type=jnp.float32)
        left_v = jnp.concatenate([lv[rows, :], rv[rows, :]], axis=0)
        gram_v = lax.dot_general(left_v, lv[cols, :], NT, preferred_element_type=jnp.float32)
        both = gram_u * gram_v
        return (both[:ROWS] - both[ROWS:]) * jnp.float32(1.0 / (NSRC * NRCV))

    def to_sibling(half, j):
        return pltpu.make_async_remote_copy(
            src_ref=send_a.at[half, j],
            dst_ref=recv_a.at[half, j],
            send_sem=a_send.at[half, j],
            recv_sem=a_recv.at[half, j],
            device_id=sibling,
            device_id_type=MESH,
        )

    def to_across(j):
        return pltpu.make_async_remote_copy(
            src_ref=send_y.at[j],
            dst_ref=recv_y.at[j],
            send_sem=y_send.at[j],
            recv_sem=y_recv.at[j],
            device_id=across,
            device_id_type=MESH,
        )

    @pl.loop(0, BLOCKS)
    def _(j):
        send_a[0, j] = term((1 - chip) * 2 + 1 - core, j).astype(jnp.bfloat16)
        to_sibling(0, j).start()

    @pl.loop(0, BLOCKS)
    def _(j):
        own = term((1 - chip) * 2 + core, j)
        to_sibling(0, j).wait_recv()
        send_y[j] = (own + recv_a[0, j].astype(jnp.float32)).astype(jnp.bfloat16)
        to_across(j).start()

    @pl.loop(0, BLOCKS)
    def _(j):
        send_a[1, j] = term(chip * 2 + 1 - core, j).astype(jnp.bfloat16)
        to_sibling(1, j).start()

    @pl.loop(0, BLOCKS)
    def _(j):
        own = term(chip * 2 + core, j)
        to_sibling(1, j).wait_recv()
        cols = pl.ds(pl.multiple_of(j * ROWS, ROWS), ROWS)
        out_ref[:, cols] = own + recv_a[1, j].astype(jnp.float32)

    @pl.loop(0, BLOCKS)
    def _(j):
        to_across(j).wait_recv()
        cols = pl.ds(pl.multiple_of(j * ROWS, ROWS), ROWS)
        out_ref[:, cols] = out_ref[:, cols] + recv_y[j].astype(jnp.float32)

    for k in range(SWEEPS):
        for face in range(6):

            @pl.when(valid[face])
            def _():
                outward(k, face).wait_send()

    @pl.loop(0, BLOCKS)
    def _(j):
        to_sibling(0, j).wait_send()
        to_sibling(1, j).wait_send()
        to_across(j).wait_send()


def local(impedance, interior_map, source_cells, receiver_cells):
    nsub = lax.axis_size("sub")
    cells = jnp.concatenate([source_cells, receiver_cells])
    bf16 = jnp.bfloat16
    vmem = pl.BlockSpec(memory_space=pltpu.VMEM)
    anywhere = pl.BlockSpec(memory_space=pl.ANY)

    def body(*refs):
        kernel(nsub, *refs)

    owned = pl.pallas_call(
        body,
        name="schwarz_hessian",
        out_shape=jax.ShapeDtypeStruct((ROWS, CELLS), jnp.float32),
        in_specs=[vmem, vmem, anywhere, anywhere],
        out_specs=vmem,
        scratch_shapes=[
            pltpu.VMEM((TRACE, TRACE), jnp.float32),
            pltpu.VMEM((TRACE, TRACE), bf16),
            pltpu.VMEM((2 * CELLS, TRACE), bf16),
            pltpu.VMEM((SWEEPS, 2, FACES, RHS), bf16),
            pltpu.VMEM((SWEEPS, 2, FACES, RHS), bf16),
            pltpu.VMEM((CELLS, RHS), bf16),
            pltpu.VMEM((CELLS, RHS), bf16),
            pltpu.VMEM((CELLS, RHS), bf16),
            pltpu.VMEM((CELLS, RHS), bf16),
            pltpu.VMEM((2, BLOCKS, ROWS, ROWS), bf16),
            pltpu.VMEM((2, BLOCKS, ROWS, ROWS), bf16),
            pltpu.VMEM((BLOCKS, ROWS, ROWS), bf16),
            pltpu.VMEM((BLOCKS, ROWS, ROWS), bf16),
            pltpu.SemaphoreType.DMA((3,)),
            pltpu.SemaphoreType.DMA((SWEEPS, 6)),
            pltpu.SemaphoreType.DMA((SWEEPS, 6)),
            pltpu.SemaphoreType.DMA((2, BLOCKS)),
            pltpu.SemaphoreType.DMA((2, BLOCKS)),
            pltpu.SemaphoreType.DMA((BLOCKS,)),
            pltpu.SemaphoreType.DMA((BLOCKS,)),
        ],
        compiler_params=pltpu.CompilerParams(
            collective_id=0, has_side_effects=True, vmem_limit_bytes=60 * 1024 * 1024
        ),
    )(cells[None, :], cells[:, None], impedance[0, 0], interior_map[0, 0])
    return owned[None]


def solution(mesh):
    in_specs = (P("freq", "sub", None, None), P("freq", "sub", None, None), P(), P())
    out_specs = P("sub", "freq", None)
    return jax.shard_map(local, mesh=mesh, in_specs=in_specs, out_specs=out_specs, check_vma=False)
```

```python
import jax
import jax.numpy as jnp
from jax import lax
from jax.experimental import pallas as pl
from jax.experimental.pallas import tpu as pltpu
from jax.sharding import PartitionSpec as P

CX = 8
CY = 8
CZ = 16
NSRC = 128
NRCV = 128
SWEEPS = 3
CELLS = 1024
FACES = 640
TRACE = 1280
RHS = 256
ROWS = 256
BLOCKS = CELLS // ROWS
MESH = pl.DeviceIdType.MESH
COUNTS = (CY * CZ, CY * CZ, CX * CZ, CX * CZ, CX * CY, CX * CY)
BEGINS = tuple(sum(COUNTS[:i]) for i in range(6))
PARTNER = (1, 0, 3, 2, 5, 4)
ORDER = (2, 3, 0, 1, 4, 5)
NT = (((1,), (1,)), ((), ()))


def kernel(
    nsub,
    source_cells,
    receiver_cells,
    z_hbm,
    interior_hbm,
    out_ref,
    zf,
    zb,
    interior,
    inc,
    outb,
    lu,
    ru,
    lv,
    rv,
    send_a,
    recv_a,
    send_y,
    recv_y,
    load_sem,
    face_send,
    face_recv,
    a_send,
    a_recv,
    y_send,
    y_recv,
):
    sub = lax.axis_index("sub")
    freq = lax.axis_index("freq")
    grid_x = min(4, nsub)
    grid_y = min(4, nsub // grid_x)
    grid_z = nsub // (grid_x * grid_y)
    sizes = (grid_x, grid_y, grid_z)
    strides = (1, grid_x, grid_x * grid_y)
    coords = (sub % grid_x, sub // grid_x % grid_y, sub // (grid_x * grid_y))
    valid = []
    beside = []
    for face in range(6):
        axis = face // 2
        if face % 2 == 0:
            valid.append(coords[axis] > 0)
            beside.append(sub - strides[axis])
        else:
            valid.append(coords[axis] < sizes[axis] - 1)
            beside.append(sub + strides[axis])
    chip = freq // 2
    core = freq % 2
    sibling = {"freq": chip * 2 + 1 - core}
    across = {"freq": (1 - chip) * 2 + core}

    def fetch(part):
        rows = pl.ds(part * CELLS, CELLS)
        return pltpu.make_async_copy(interior_hbm.at[rows], interior.at[rows], load_sem.at[part])

    fetch_z = pltpu.make_async_copy(z_hbm, zf, load_sem.at[2])
    fetch(0).start()
    fetch_z.start()
    fetch(1).start()

    barrier = pltpu.get_barrier_semaphore()
    greeted = jnp.int32(2)
    for face in range(6):
        greeted = greeted + valid[face].astype(jnp.int32)

        @pl.when(valid[face])
        def _():
            pl.semaphore_signal(barrier, inc=1, device_id={"sub": beside[face]}, device_id_type=MESH)

    pl.semaphore_signal(barrier, inc=1, device_id=sibling, device_id_type=MESH)
    pl.semaphore_signal(barrier, inc=1, device_id=across, device_id_type=MESH)

    def span(face):
        return pl.ds(BEGINS[face], COUNTS[face])

    for face in range(6):

        @pl.when(jnp.logical_not(valid[face]))
        def _():
            for k in range(SWEEPS):
                inc[k, :, :, span(face), :] = jnp.zeros((2, 2, COUNTS[face], NSRC), jnp.bfloat16)

    def outward(k, half, face):
        other = PARTNER[face]
        return pltpu.make_async_remote_copy(
            src_ref=outb.at[k, half, :, span(face), :],
            dst_ref=inc.at[k, half, :, span(other), :],
            send_sem=face_send.at[k, half, face],
            recv_sem=face_recv.at[k, half, other],
            device_id={"sub": beside[face]},
            device_id_type=MESH,
        )

    def inward(k, half, face):
        return pltpu.make_async_remote_copy(
            src_ref=outb.at[k, half, :, span(face), :],
            dst_ref=inc.at[k, half, :, span(face), :],
            send_sem=face_send.at[k, half, face],
            recv_sem=face_recv.at[k, half, face],
            device_id={"sub": beside[face]},
            device_id_type=MESH,
        )

    def send(k, half, face):
        @pl.when(valid[face])
        def _():
            outward(k, half, face).start()

    def receive(k, half):
        for face in ORDER:

            @pl.when(valid[face])
            def _():
                inward(k, half, face).wait_recv()

    first = sub * CELLS
    for half, cells in enumerate((source_cells, receiver_cells)):
        column = jnp.broadcast_to(cells[...] - first, (NSRC, NSRC)).T
        lanes = lax.broadcasted_iota(jnp.int32, (NSRC, NSRC), 1)
        hot = jnp.concatenate([(column == lanes + i * NSRC).astype(jnp.float32) for i in range(CELLS // NSRC)], axis=1)
        if half == 0:
            fetch(0).wait()
        picked = jnp.dot(hot.astype(jnp.bfloat16), interior[:CELLS, :], preferred_element_type=jnp.float32)
        load = picked.T.astype(jnp.bfloat16)
        outb[0, half, 0] = load[:FACES]
        outb[0, half, 1] = load[FACES:]
        if half == 0:
            pl.semaphore_wait(barrier, greeted)
        for face in ORDER:
            send(0, half, face)

    fetch_z.wait()

    @pl.loop(0, TRACE // 128)
    def _(i):
        rows = pl.ds(pl.multiple_of(i * 128, 128), 128)
        zb[rows, :] = zf[rows, :].astype(jnp.bfloat16)

    for k in range(1, SWEEPS):
        for half in range(2):
            receive(k - 1, half)
            arrived = inc[k - 1, half].reshape(TRACE, NSRC)
            for face in ORDER[::2]:
                begin = BEGINS[face]
                count = COUNTS[face] * 2
                z_rows = jnp.concatenate(
                    [zb[begin : begin + count, :], zb[FACES + begin : FACES + begin + count, :]], axis=0
                )
                product = jnp.dot(z_rows, arrived, preferred_element_type=jnp.float32)
                for part in range(2):
                    added = outb[0, half, part, begin : begin + count, :].astype(jnp.float32)
                    total = product[part * count : (part + 1) * count] + added
                    outb[k, half, part, begin : begin + count, :] = total.astype(jnp.bfloat16)
                send(k, half, face)
                send(k, half, face + 1)
    fetch(1).wait()

    field_scale = jnp.float32(TRACE ** (-0.5))

    for half, cells, left, right in ((0, source_cells, lu, ru), (1, receiver_cells, lv, rv)):
        receive(SWEEPS - 1, half)

        @pl.loop(0, BLOCKS)
        def _(i):
            begin = pl.multiple_of(i * ROWS, ROWS)
            trace = inc[SWEEPS - 1, half].reshape(TRACE, NSRC)
            rows = pl.ds(begin, ROWS)
            real = jnp.dot(interior[rows, :], trace, preferred_element_type=jnp.float32)
            low = pl.ds(pl.multiple_of(CELLS + i * ROWS, ROWS), ROWS)
            imag = jnp.dot(interior[low, :], trace, preferred_element_type=jnp.float32)
            point = cells[...] == first + begin + lax.broadcasted_iota(jnp.int32, (ROWS, NSRC), 0)
            real = real * field_scale + point.astype(jnp.float32)
            imag = imag * field_scale
            left[rows, :NSRC] = real.astype(jnp.bfloat16)
            left[rows, NSRC:] = imag.astype(jnp.bfloat16)
            right[rows, :NSRC] = imag.astype(jnp.bfloat16)
            right[rows, NSRC:] = (-real).astype(jnp.bfloat16)

    def term(owner, j):
        rows = pl.ds(pl.multiple_of(owner * ROWS, ROWS), ROWS)
        cols = pl.ds(pl.multiple_of(j * ROWS, ROWS), ROWS)
        left_u = jnp.concatenate([lu[rows, :], ru[rows, :]], axis=0)
        gram_u = lax.dot_general(left_u, lu[cols, :], NT, preferred_element_type=jnp.float32)
        left_v = jnp.concatenate([lv[rows, :], rv[rows, :]], axis=0)
        gram_v = lax.dot_general(left_v, lv[cols, :], NT, preferred_element_type=jnp.float32)
        both = gram_u * gram_v
        return (both[:ROWS] - both[ROWS:]) * jnp.float32(1.0 / (NSRC * NRCV))

    def to_sibling(half, j):
        return pltpu.make_async_remote_copy(
            src_ref=send_a.at[half, j],
            dst_ref=recv_a.at[half, j],
            send_sem=a_send.at[half, j],
            recv_sem=a_recv.at[half, j],
            device_id=sibling,
            device_id_type=MESH,
        )

    def to_across(j):
        return pltpu.make_async_remote_copy(
            src_ref=send_y.at[j],
            dst_ref=recv_y.at[j],
            send_sem=y_send.at[j],
            recv_sem=y_recv.at[j],
            device_id=across,
            device_id_type=MESH,
        )

    def give(half, j):
        owner = (1 - chip + half * (2 * chip - 1)) * 2 + 1 - core
        send_a[half, j] = term(owner, j).astype(jnp.bfloat16)
        to_sibling(half, j).start()

    def pass_on(j):
        own = term((1 - chip) * 2 + core, j)
        to_sibling(0, j).wait_recv()
        send_y[j] = (own + recv_a[0, j].astype(jnp.float32)).astype(jnp.bfloat16)
        to_across(j).start()

    give(0, 0)

    @pl.loop(0, BLOCKS - 1)
    def _(j):
        give(0, j + 1)
        pass_on(j)

    pass_on(BLOCKS - 1)

    @pl.loop(0, BLOCKS)
    def _(j):
        give(1, j)

    @pl.loop(0, BLOCKS)
    def _(j):
        own = term(chip * 2 + core, j)
        to_sibling(1, j).wait_recv()
        cols = pl.ds(pl.multiple_of(j * ROWS, ROWS), ROWS)
        out_ref[:, cols] = own + recv_a[1, j].astype(jnp.float32)

    @pl.loop(0, BLOCKS)
    def _(j):
        to_across(j).wait_recv()
        cols = pl.ds(pl.multiple_of(j * ROWS, ROWS), ROWS)
        out_ref[:, cols] = out_ref[:, cols] + recv_y[j].astype(jnp.float32)

    for k in range(SWEEPS):
        for face in range(6):

            @pl.when(valid[face])
            def _():
                for half in range(2):
                    outward(k, half, face).wait_send()

    @pl.loop(0, BLOCKS)
    def _(j):
        to_sibling(0, j).wait_send()
        to_sibling(1, j).wait_send()
        to_across(j).wait_send()


def local(impedance, interior_map, source_cells, receiver_cells):
    nsub = lax.axis_size("sub")
    bf16 = jnp.bfloat16
    vmem = pl.BlockSpec(memory_space=pltpu.VMEM)
    anywhere = pl.BlockSpec(memory_space=pltpu.HBM)

    def body(*refs):
        kernel(nsub, *refs)

    owned = pl.pallas_call(
        body,
        name="schwarz_hessian",
        out_shape=jax.ShapeDtypeStruct((ROWS, CELLS), jnp.float32),
        in_specs=[vmem, vmem, anywhere, anywhere],
        out_specs=vmem,
        scratch_shapes=[
            pltpu.VMEM((TRACE, TRACE), jnp.float32),
            pltpu.VMEM((TRACE, TRACE), bf16),
            pltpu.VMEM((2 * CELLS, TRACE), bf16),
            pltpu.VMEM((SWEEPS, 2, 2, FACES, NSRC), bf16),
            pltpu.VMEM((SWEEPS, 2, 2, FACES, NSRC), bf16),
            pltpu.VMEM((CELLS, RHS), bf16),
            pltpu.VMEM((CELLS, RHS), bf16),
            pltpu.VMEM((CELLS, RHS), bf16),
            pltpu.VMEM((CELLS, RHS), bf16),
            pltpu.VMEM((2, BLOCKS, ROWS, ROWS), bf16),
            pltpu.VMEM((2, BLOCKS, ROWS, ROWS), bf16),
            pltpu.VMEM((BLOCKS, ROWS, ROWS), bf16),
            pltpu.VMEM((BLOCKS, ROWS, ROWS), bf16),
            pltpu.SemaphoreType.DMA((3,)),
            pltpu.SemaphoreType.DMA((SWEEPS, 2, 6)),
            pltpu.SemaphoreType.DMA((SWEEPS, 2, 6)),
            pltpu.SemaphoreType.DMA((2, BLOCKS)),
            pltpu.SemaphoreType.DMA((2, BLOCKS)),
            pltpu.SemaphoreType.DMA((BLOCKS,)),
            pltpu.SemaphoreType.DMA((BLOCKS,)),
        ],
        compiler_params=pltpu.CompilerParams(
            collective_id=0, has_side_effects=True, vmem_limit_bytes=59 * 1024 * 1024
        ),
    )(source_cells[None, :], receiver_cells[None, :], impedance[0, 0], interior_map[0, 0])
    return owned[None]


def solution(mesh):
    in_specs = (P("freq", "sub", None, None), P("freq", "sub", None, None), P(), P())
    out_specs = P("sub", "freq", None)
    return jax.shard_map(local, mesh=mesh, in_specs=in_specs, out_specs=out_specs, check_vma=False)
```

```python
import jax
import jax.numpy as jnp
from jax import lax
from jax.experimental import pallas as pl
from jax.experimental.pallas import tpu as pltpu
from jax.sharding import PartitionSpec as P

CX = 8
CY = 8
CZ = 16
NSRC = 128
NRCV = 128
SWEEPS = 3
CELLS = 1024
FACES = 640
TRACE = 1280
RHS = 256
ROWS = 256
BLOCKS = CELLS // ROWS
MESH = pl.DeviceIdType.MESH
COUNTS = (CY * CZ, CY * CZ, CX * CZ, CX * CZ, CX * CY, CX * CY)
BEGINS = tuple(sum(COUNTS[:i]) for i in range(6))
PARTNER = (1, 0, 3, 2, 5, 4)
ORDER = (2, 3, 0, 1, 4, 5)
NT = (((1,), (1,)), ((), ()))


def kernel(
    nsub,
    source_cells,
    receiver_cells,
    z_hbm,
    interior_hbm,
    out_ref,
    zf,
    zb,
    interior,
    inc,
    outb,
    lu,
    ru,
    lv,
    rv,
    send_a,
    recv_a,
    send_y,
    recv_y,
    load_sem,
    face_send,
    face_recv,
    a_send,
    a_recv,
    y_send,
    y_recv,
):
    sub = lax.axis_index("sub")
    freq = lax.axis_index("freq")
    grid_x = min(4, nsub)
    grid_y = min(4, nsub // grid_x)
    grid_z = nsub // (grid_x * grid_y)
    sizes = (grid_x, grid_y, grid_z)
    strides = (1, grid_x, grid_x * grid_y)
    coords = (sub % grid_x, sub // grid_x % grid_y, sub // (grid_x * grid_y))
    valid = []
    beside = []
    for face in range(6):
        axis = face // 2
        if face % 2 == 0:
            valid.append(coords[axis] > 0)
            beside.append(sub - strides[axis])
        else:
            valid.append(coords[axis] < sizes[axis] - 1)
            beside.append(sub + strides[axis])
    chip = freq // 2
    core = freq % 2
    sibling = {"freq": chip * 2 + 1 - core}
    across = {"freq": (1 - chip) * 2 + core}

    def fetch(part):
        rows = pl.ds(part * CELLS, CELLS)
        return pltpu.make_async_copy(interior_hbm.at[rows], interior.at[rows], load_sem.at[part])

    fetch_z = pltpu.make_async_copy(z_hbm, zf, load_sem.at[2])
    fetch(0).start()

    barrier = pltpu.get_barrier_semaphore()
    greeted = jnp.int32(2)
    for face in range(6):
        greeted = greeted + valid[face].astype(jnp.int32)

        @pl.when(valid[face])
        def _():
            pl.semaphore_signal(barrier, inc=1, device_id={"sub": beside[face]}, device_id_type=MESH)

    pl.semaphore_signal(barrier, inc=1, device_id=sibling, device_id_type=MESH)
    pl.semaphore_signal(barrier, inc=1, device_id=across, device_id_type=MESH)

    def span(face):
        return pl.ds(BEGINS[face], COUNTS[face])

    for face in range(6):

        @pl.when(jnp.logical_not(valid[face]))
        def _():
            for k in range(SWEEPS):
                inc[k, :, :, span(face), :] = jnp.zeros((2, 2, COUNTS[face], NSRC), jnp.bfloat16)

    def outward(k, half, face):
        other = PARTNER[face]
        return pltpu.make_async_remote_copy(
            src_ref=outb.at[k, half, :, span(face), :],
            dst_ref=inc.at[k, half, :, span(other), :],
            send_sem=face_send.at[k, half, face],
            recv_sem=face_recv.at[k, half, other],
            device_id={"sub": beside[face]},
            device_id_type=MESH,
        )

    def inward(k, half, face):
        return pltpu.make_async_remote_copy(
            src_ref=outb.at[k, half, :, span(face), :],
            dst_ref=inc.at[k, half, :, span(face), :],
            send_sem=face_send.at[k, half, face],
            recv_sem=face_recv.at[k, half, face],
            device_id={"sub": beside[face]},
            device_id_type=MESH,
        )

    def send(k, half, face):
        @pl.when(valid[face])
        def _():
            outward(k, half, face).start()

    def receive(k, half):
        for face in ORDER:

            @pl.when(valid[face])
            def _():
                inward(k, half, face).wait_recv()

    first = sub * CELLS
    for half, cells in enumerate((source_cells, receiver_cells)):
        column = jnp.broadcast_to(cells[...] - first, (NSRC, NSRC)).T
        lanes = lax.broadcasted_iota(jnp.int32, (NSRC, NSRC), 1)
        hot = jnp.concatenate([(column == lanes + i * NSRC).astype(jnp.float32) for i in range(CELLS // NSRC)], axis=1)
        if half == 0:
            fetch(0).wait()
            fetch_z.start()
            fetch(1).start()
        picked = jnp.dot(hot.astype(jnp.bfloat16), interior[:CELLS, :], preferred_element_type=jnp.float32)
        load = picked.T.astype(jnp.bfloat16)
        outb[0, half, 0] = load[:FACES]
        outb[0, half, 1] = load[FACES:]
        if half == 0:
            pl.semaphore_wait(barrier, greeted)
        for face in ORDER:
            send(0, half, face)

    fetch_z.wait()

    @pl.loop(0, TRACE // 128)
    def _(i):
        rows = pl.ds(pl.multiple_of(i * 128, 128), 128)
        zb[rows, :] = zf[rows, :].astype(jnp.bfloat16)

    for k in range(1, SWEEPS):
        for half in range(2):
            receive(k - 1, half)
            arrived = inc[k - 1, half].reshape(TRACE, NSRC)
            for face in ORDER[::2]:
                begin = BEGINS[face]
                count = COUNTS[face] * 2
                z_rows = jnp.concatenate(
                    [zb[begin : begin + count, :], zb[FACES + begin : FACES + begin + count, :]], axis=0
                )
                product = jnp.dot(z_rows, arrived, preferred_element_type=jnp.float32)
                for part in range(2):
                    added = outb[0, half, part, begin : begin + count, :].astype(jnp.float32)
                    total = product[part * count : (part + 1) * count] + added
                    outb[k, half, part, begin : begin + count, :] = total.astype(jnp.bfloat16)
                send(k, half, face)
                send(k, half, face + 1)
    fetch(1).wait()

    field_scale = jnp.float32(TRACE ** (-0.5))

    for half, cells, left, right in ((0, source_cells, lu, ru), (1, receiver_cells, lv, rv)):
        receive(SWEEPS - 1, half)

        @pl.loop(0, BLOCKS)
        def _(i):
            begin = pl.multiple_of(i * ROWS, ROWS)
            trace = inc[SWEEPS - 1, half].reshape(TRACE, NSRC)
            rows = pl.ds(begin, ROWS)
            real = jnp.dot(interior[rows, :], trace, preferred_element_type=jnp.float32)
            low = pl.ds(pl.multiple_of(CELLS + i * ROWS, ROWS), ROWS)
            imag = jnp.dot(interior[low, :], trace, preferred_element_type=jnp.float32)
            point = cells[...] == first + begin + lax.broadcasted_iota(jnp.int32, (ROWS, NSRC), 0)
            real = real * field_scale + point.astype(jnp.float32)
            imag = imag * field_scale
            left[rows, :NSRC] = real.astype(jnp.bfloat16)
            left[rows, NSRC:] = imag.astype(jnp.bfloat16)
            right[rows, :NSRC] = imag.astype(jnp.bfloat16)
            right[rows, NSRC:] = (-real).astype(jnp.bfloat16)

    def term(owner, j):
        rows = pl.ds(pl.multiple_of(owner * ROWS, ROWS), ROWS)
        cols = pl.ds(pl.multiple_of(j * ROWS, ROWS), ROWS)
        left_u = jnp.concatenate([lu[rows, :], ru[rows, :]], axis=0)
        gram_u = lax.dot_general(left_u, lu[cols, :], NT, preferred_element_type=jnp.float32)
        left_v = jnp.concatenate([lv[rows, :], rv[rows, :]], axis=0)
        gram_v = lax.dot_general(left_v, lv[cols, :], NT, preferred_element_type=jnp.float32)
        both = gram_u * gram_v
        return (both[:ROWS] - both[ROWS:]) * jnp.float32(1.0 / (NSRC * NRCV))

    def to_sibling(half, j):
        return pltpu.make_async_remote_copy(
            src_ref=send_a.at[half, j],
            dst_ref=recv_a.at[half, j],
            send_sem=a_send.at[half, j],
            recv_sem=a_recv.at[half, j],
            device_id=sibling,
            device_id_type=MESH,
        )

    def to_across(j):
        return pltpu.make_async_remote_copy(
            src_ref=send_y.at[j],
            dst_ref=recv_y.at[j],
            send_sem=y_send.at[j],
            recv_sem=y_recv.at[j],
            device_id=across,
            device_id_type=MESH,
        )

    def give(half, j):
        owner = (1 - chip + half * (2 * chip - 1)) * 2 + 1 - core
        send_a[half, j] = term(owner, j).astype(jnp.bfloat16)
        to_sibling(half, j).start()

    def pass_on(j):
        own = term((1 - chip) * 2 + core, j)
        to_sibling(0, j).wait_recv()
        send_y[j] = (own + recv_a[0, j].astype(jnp.float32)).astype(jnp.bfloat16)
        to_across(j).start()

    give(0, 0)

    @pl.loop(0, BLOCKS - 1)
    def _(j):
        give(0, j + 1)
        pass_on(j)

    pass_on(BLOCKS - 1)

    @pl.loop(0, BLOCKS)
    def _(j):
        give(1, j)

    @pl.loop(0, BLOCKS)
    def _(j):
        own = term(chip * 2 + core, j)
        to_sibling(1, j).wait_recv()
        cols = pl.ds(pl.multiple_of(j * ROWS, ROWS), ROWS)
        out_ref[:, cols] = own + recv_a[1, j].astype(jnp.float32)

    @pl.loop(0, BLOCKS)
    def _(j):
        to_across(j).wait_recv()
        cols = pl.ds(pl.multiple_of(j * ROWS, ROWS), ROWS)
        out_ref[:, cols] = out_ref[:, cols] + recv_y[j].astype(jnp.float32)

    for k in range(SWEEPS):
        for face in range(6):

            @pl.when(valid[face])
            def _():
                for half in range(2):
                    outward(k, half, face).wait_send()

    @pl.loop(0, BLOCKS)
    def _(j):
        to_sibling(0, j).wait_send()
        to_sibling(1, j).wait_send()
        to_across(j).wait_send()


def local(impedance, interior_map, source_cells, receiver_cells):
    nsub = lax.axis_size("sub")
    bf16 = jnp.bfloat16
    vmem = pl.BlockSpec(memory_space=pltpu.VMEM)
    anywhere = pl.BlockSpec(memory_space=pltpu.HBM)

    def body(*refs):
        kernel(nsub, *refs)

    owned = pl.pallas_call(
        body,
        name="schwarz_hessian",
        out_shape=jax.ShapeDtypeStruct((ROWS, CELLS), jnp.float32),
        in_specs=[vmem, vmem, anywhere, anywhere],
        out_specs=vmem,
        scratch_shapes=[
            pltpu.VMEM((TRACE, TRACE), jnp.float32),
            pltpu.VMEM((TRACE, TRACE), bf16),
            pltpu.VMEM((2 * CELLS, TRACE), bf16),
            pltpu.VMEM((SWEEPS, 2, 2, FACES, NSRC), bf16),
            pltpu.VMEM((SWEEPS, 2, 2, FACES, NSRC), bf16),
            pltpu.VMEM((CELLS, RHS), bf16),
            pltpu.VMEM((CELLS, RHS), bf16),
            pltpu.VMEM((CELLS, RHS), bf16),
            pltpu.VMEM((CELLS, RHS), bf16),
            pltpu.VMEM((2, BLOCKS, ROWS, ROWS), bf16),
            pltpu.VMEM((2, BLOCKS, ROWS, ROWS), bf16),
            pltpu.VMEM((BLOCKS, ROWS, ROWS), bf16),
            pltpu.VMEM((BLOCKS, ROWS, ROWS), bf16),
            pltpu.SemaphoreType.DMA((3,)),
            pltpu.SemaphoreType.DMA((SWEEPS, 2, 6)),
            pltpu.SemaphoreType.DMA((SWEEPS, 2, 6)),
            pltpu.SemaphoreType.DMA((2, BLOCKS)),
            pltpu.SemaphoreType.DMA((2, BLOCKS)),
            pltpu.SemaphoreType.DMA((BLOCKS,)),
            pltpu.SemaphoreType.DMA((BLOCKS,)),
        ],
        compiler_params=pltpu.CompilerParams(
            collective_id=0, has_side_effects=True, vmem_limit_bytes=52 * 1024 * 1024
        ),
    )(source_cells[None, :], receiver_cells[None, :], impedance[0, 0], interior_map[0, 0])
    return owned[None]


def solution(mesh):
    in_specs = (P("freq", "sub", None, None), P("freq", "sub", None, None), P(), P())
    out_specs = P("sub", "freq", None)
    return jax.shard_map(local, mesh=mesh, in_specs=in_specs, out_specs=out_specs, check_vma=False)
```

```python
import jax
import jax.numpy as jnp
from jax import lax
from jax.experimental import pallas as pl
from jax.experimental.pallas import tpu as pltpu
from jax.sharding import PartitionSpec as P

CX = 8
CY = 8
CZ = 16
NSRC = 128
NRCV = 128
SWEEPS = 3
CELLS = 1024
FACES = 640
TRACE = 1280
RHS = 256
ROWS = 256
BLOCKS = CELLS // ROWS
MESH = pl.DeviceIdType.MESH
COUNTS = (CY * CZ, CY * CZ, CX * CZ, CX * CZ, CX * CY, CX * CY)
BEGINS = tuple(sum(COUNTS[:i]) for i in range(6))
PARTNER = (1, 0, 3, 2, 5, 4)
ORDER = (2, 3, 0, 1, 4, 5)
NT = (((1,), (1,)), ((), ()))


def kernel(
    nsub,
    source_cells,
    receiver_cells,
    z_hbm,
    interior_hbm,
    out_ref,
    zf,
    zb,
    interior,
    inc,
    outb,
    lu,
    ru,
    lv,
    rv,
    send_a,
    recv_a,
    send_y,
    recv_y,
    load_sem,
    face_send,
    face_recv,
    a_send,
    a_recv,
    y_send,
    y_recv,
):
    sub = lax.axis_index("sub")
    freq = lax.axis_index("freq")
    grid_x = min(4, nsub)
    grid_y = min(4, nsub // grid_x)
    grid_z = nsub // (grid_x * grid_y)
    sizes = (grid_x, grid_y, grid_z)
    strides = (1, grid_x, grid_x * grid_y)
    coords = (sub % grid_x, sub // grid_x % grid_y, sub // (grid_x * grid_y))
    valid = []
    beside = []
    for face in range(6):
        axis = face // 2
        if face % 2 == 0:
            valid.append(coords[axis] > 0)
            beside.append(sub - strides[axis])
        else:
            valid.append(coords[axis] < sizes[axis] - 1)
            beside.append(sub + strides[axis])
    chip = freq // 2
    core = freq % 2
    sibling = {"freq": chip * 2 + 1 - core}
    across = {"freq": (1 - chip) * 2 + core}

    def fetch(part):
        rows = pl.ds(part * CELLS, CELLS)
        return pltpu.make_async_copy(interior_hbm.at[rows], interior.at[rows], load_sem.at[part])

    fetch_z = pltpu.make_async_copy(z_hbm, zf, load_sem.at[2])
    fetch(0).start()

    barrier = pltpu.get_barrier_semaphore()
    greeted = jnp.int32(2)
    for face in range(6):
        greeted = greeted + valid[face].astype(jnp.int32)

        @pl.when(valid[face])
        def _():
            pl.semaphore_signal(barrier, inc=1, device_id={"sub": beside[face]}, device_id_type=MESH)

    pl.semaphore_signal(barrier, inc=1, device_id=sibling, device_id_type=MESH)
    pl.semaphore_signal(barrier, inc=1, device_id=across, device_id_type=MESH)

    def span(face):
        return pl.ds(BEGINS[face], COUNTS[face])

    for face in range(6):

        @pl.when(jnp.logical_not(valid[face]))
        def _():
            for k in range(SWEEPS):
                inc[k, :, :, span(face), :] = jnp.zeros((2, 2, COUNTS[face], NSRC), jnp.bfloat16)

    def outward(k, half, face):
        other = PARTNER[face]
        return pltpu.make_async_remote_copy(
            src_ref=outb.at[k, half, :, span(face), :],
            dst_ref=inc.at[k, half, :, span(other), :],
            send_sem=face_send.at[k, half, face],
            recv_sem=face_recv.at[k, half, other],
            device_id={"sub": beside[face]},
            device_id_type=MESH,
        )

    def inward(k, half, face):
        return pltpu.make_async_remote_copy(
            src_ref=outb.at[k, half, :, span(face), :],
            dst_ref=inc.at[k, half, :, span(face), :],
            send_sem=face_send.at[k, half, face],
            recv_sem=face_recv.at[k, half, face],
            device_id={"sub": beside[face]},
            device_id_type=MESH,
        )

    def send(k, half, face):
        @pl.when(valid[face])
        def _():
            outward(k, half, face).start()

    def receive(k, half):
        for face in ORDER:

            @pl.when(valid[face])
            def _():
                inward(k, half, face).wait_recv()

    first = sub * CELLS
    for half, cells in enumerate((source_cells, receiver_cells)):
        column = jnp.broadcast_to(cells[...] - first, (NSRC, NSRC)).T
        lanes = lax.broadcasted_iota(jnp.int32, (NSRC, NSRC), 1)
        hot = jnp.concatenate([(column == lanes + i * NSRC).astype(jnp.float32) for i in range(CELLS // NSRC)], axis=1)
        if half == 0:
            fetch(0).wait()
            fetch_z.start()
            fetch(1).start()
        hot = hot.astype(jnp.bfloat16)
        for axis in (1, 0, 2):
            begin = BEGINS[2 * axis]
            count = COUNTS[2 * axis] * 2
            for part in range(2):
                columns = slice(part * FACES + begin, part * FACES + begin + count)
                picked = jnp.dot(hot, interior[:CELLS, columns], preferred_element_type=jnp.float32)
                outb[0, half, part, begin : begin + count, :] = picked.T.astype(jnp.bfloat16)
            if half == 0 and axis == 1:
                pl.semaphore_wait(barrier, greeted)
            send(0, half, 2 * axis)
            send(0, half, 2 * axis + 1)

    fetch_z.wait()

    @pl.loop(0, TRACE // 128)
    def _(i):
        rows = pl.ds(pl.multiple_of(i * 128, 128), 128)
        zb[rows, :] = zf[rows, :].astype(jnp.bfloat16)

    for k in range(1, SWEEPS):
        for half in range(2):
            receive(k - 1, half)
            arrived = inc[k - 1, half].reshape(TRACE, NSRC)
            for face in ORDER[::2]:
                begin = BEGINS[face]
                count = COUNTS[face] * 2
                z_rows = jnp.concatenate(
                    [zb[begin : begin + count, :], zb[FACES + begin : FACES + begin + count, :]], axis=0
                )
                product = jnp.dot(z_rows, arrived, preferred_element_type=jnp.float32)
                for part in range(2):
                    added = outb[0, half, part, begin : begin + count, :].astype(jnp.float32)
                    total = product[part * count : (part + 1) * count] + added
                    outb[k, half, part, begin : begin + count, :] = total.astype(jnp.bfloat16)
                send(k, half, face)
                send(k, half, face + 1)
    fetch(1).wait()

    field_scale = jnp.float32(TRACE ** (-0.5))

    for half, cells, left, right in ((0, source_cells, lu, ru), (1, receiver_cells, lv, rv)):
        receive(SWEEPS - 1, half)

        @pl.loop(0, BLOCKS)
        def _(i):
            begin = pl.multiple_of(i * ROWS, ROWS)
            trace = inc[SWEEPS - 1, half].reshape(TRACE, NSRC)
            rows = pl.ds(begin, ROWS)
            real = jnp.dot(interior[rows, :], trace, preferred_element_type=jnp.float32)
            low = pl.ds(pl.multiple_of(CELLS + i * ROWS, ROWS), ROWS)
            imag = jnp.dot(interior[low, :], trace, preferred_element_type=jnp.float32)
            point = cells[...] == first + begin + lax.broadcasted_iota(jnp.int32, (ROWS, NSRC), 0)
            real = real * field_scale + point.astype(jnp.float32)
            imag = imag * field_scale
            left[rows, :NSRC] = real.astype(jnp.bfloat16)
            left[rows, NSRC:] = imag.astype(jnp.bfloat16)
            right[rows, :NSRC] = imag.astype(jnp.bfloat16)
            right[rows, NSRC:] = (-real).astype(jnp.bfloat16)

    def term(owner, j):
        rows = pl.ds(pl.multiple_of(owner * ROWS, ROWS), ROWS)
        cols = pl.ds(pl.multiple_of(j * ROWS, ROWS), ROWS)
        left_u = jnp.concatenate([lu[rows, :], ru[rows, :]], axis=0)
        gram_u = lax.dot_general(left_u, lu[cols, :], NT, preferred_element_type=jnp.float32)
        left_v = jnp.concatenate([lv[rows, :], rv[rows, :]], axis=0)
        gram_v = lax.dot_general(left_v, lv[cols, :], NT, preferred_element_type=jnp.float32)
        both = gram_u * gram_v
        return (both[:ROWS] - both[ROWS:]) * jnp.float32(1.0 / (NSRC * NRCV))

    def to_sibling(half, j):
        return pltpu.make_async_remote_copy(
            src_ref=send_a.at[half, j],
            dst_ref=recv_a.at[half, j],
            send_sem=a_send.at[half, j],
            recv_sem=a_recv.at[half, j],
            device_id=sibling,
            device_id_type=MESH,
        )

    def to_across(j):
        return pltpu.make_async_remote_copy(
            src_ref=send_y.at[j],
            dst_ref=recv_y.at[j],
            send_sem=y_send.at[j],
            recv_sem=y_recv.at[j],
            device_id=across,
            device_id_type=MESH,
        )

    def give(half, j):
        owner = (1 - chip + half * (2 * chip - 1)) * 2 + 1 - core
        send_a[half, j] = term(owner, j).astype(jnp.bfloat16)
        to_sibling(half, j).start()

    def pass_on(j):
        own = term((1 - chip) * 2 + core, j)
        to_sibling(0, j).wait_recv()
        send_y[j] = (own + recv_a[0, j].astype(jnp.float32)).astype(jnp.bfloat16)
        to_across(j).start()

    @pl.loop(0, BLOCKS)
    def _(j):
        give(0, j)
        pass_on(j)

    @pl.loop(0, BLOCKS)
    def _(j):
        give(1, j)

    @pl.loop(0, BLOCKS)
    def _(j):
        own = term(chip * 2 + core, j)
        to_sibling(1, j).wait_recv()
        cols = pl.ds(pl.multiple_of(j * ROWS, ROWS), ROWS)
        out_ref[:, cols] = own + recv_a[1, j].astype(jnp.float32)

    @pl.loop(0, BLOCKS)
    def _(j):
        to_across(j).wait_recv()
        cols = pl.ds(pl.multiple_of(j * ROWS, ROWS), ROWS)
        out_ref[:, cols] = out_ref[:, cols] + recv_y[j].astype(jnp.float32)

    for k in range(SWEEPS):
        for face in range(6):

            @pl.when(valid[face])
            def _():
                for half in range(2):
                    outward(k, half, face).wait_send()

    @pl.loop(0, BLOCKS)
    def _(j):
        to_sibling(0, j).wait_send()
        to_sibling(1, j).wait_send()
        to_across(j).wait_send()


def local(impedance, interior_map, source_cells, receiver_cells):
    nsub = lax.axis_size("sub")
    bf16 = jnp.bfloat16
    vmem = pl.BlockSpec(memory_space=pltpu.VMEM)
    anywhere = pl.BlockSpec(memory_space=pltpu.HBM)

    def body(*refs):
        kernel(nsub, *refs)

    owned = pl.pallas_call(
        body,
        name="schwarz_hessian",
        out_shape=jax.ShapeDtypeStruct((ROWS, CELLS), jnp.float32),
        in_specs=[vmem, vmem, anywhere, anywhere],
        out_specs=vmem,
        scratch_shapes=[
            pltpu.VMEM((TRACE, TRACE), jnp.float32),
            pltpu.VMEM((TRACE, TRACE), bf16),
            pltpu.VMEM((2 * CELLS, TRACE), bf16),
            pltpu.VMEM((SWEEPS, 2, 2, FACES, NSRC), bf16),
            pltpu.VMEM((SWEEPS, 2, 2, FACES, NSRC), bf16),
            pltpu.VMEM((CELLS, RHS), bf16),
            pltpu.VMEM((CELLS, RHS), bf16),
            pltpu.VMEM((CELLS, RHS), bf16),
            pltpu.VMEM((CELLS, RHS), bf16),
            pltpu.VMEM((2, BLOCKS, ROWS, ROWS), bf16),
            pltpu.VMEM((2, BLOCKS, ROWS, ROWS), bf16),
            pltpu.VMEM((BLOCKS, ROWS, ROWS), bf16),
            pltpu.VMEM((BLOCKS, ROWS, ROWS), bf16),
            pltpu.SemaphoreType.DMA((3,)),
            pltpu.SemaphoreType.DMA((SWEEPS, 2, 6)),
            pltpu.SemaphoreType.DMA((SWEEPS, 2, 6)),
            pltpu.SemaphoreType.DMA((2, BLOCKS)),
            pltpu.SemaphoreType.DMA((2, BLOCKS)),
            pltpu.SemaphoreType.DMA((BLOCKS,)),
            pltpu.SemaphoreType.DMA((BLOCKS,)),
        ],
        compiler_params=pltpu.CompilerParams(
            collective_id=0, has_side_effects=True, vmem_limit_bytes=52 * 1024 * 1024
        ),
    )(source_cells[None, :], receiver_cells[None, :], impedance[0, 0], interior_map[0, 0])
    return owned[None]


def solution(mesh):
    in_specs = (P("freq", "sub", None, None), P("freq", "sub", None, None), P(), P())
    out_specs = P("sub", "freq", None)
    return jax.shard_map(local, mesh=mesh, in_specs=in_specs, out_specs=out_specs, check_vma=False)
```
